32 devices in a mesh: cfg: 2 (over core), seq: 8 (over z, y), mlp: 2 (over x).
Axes of the slice: x: 2, y: 2, z: 4, core: 2. Of those that a mesh axis runs over, the one named last changes fastest.
Arguments:
- image_hidden: bfloat16 [2, 256, 8, 1536], P('cfg', ('seq', 'mlp')), may hold values from -6 to 6
- text_hidden: bfloat16 [2, 1232, 1536], P('cfg', 'seq'), may hold values from -6 to 6
- modulation: float32 [2, 8, 10, 1536], P('cfg'), may hold values from -3 to 3
- text_lengths: int32 [2, 8], P('cfg'), may hold values from 1 to 154, as said below
- timestep: int32 [1], replicated, may hold values from 0 to 27
- latent: float32 [256, 8, 64], P(('seq', 'mlp'), 'cfg'), may hold values from -6 to 6
- w_qkv: bfloat16 [3, 1536, 1536], P(None, None, 'mlp'), may hold values from -0.15625 to 0.15625
- w_out: bfloat16 [1536, 1536], P('mlp'), may hold values from -0.15625 to 0.15625
- w_text_kv: bfloat16 [2, 1536, 1536], P(None, None, 'mlp'), may hold values from -0.15625 to 0.15625
- norm_gain: float32 [3, 64], replicated, may hold values from 1 to 2
- w_up: bfloat16 [1536, 6144], P(None, 'mlp'), may hold values from -0.15625 to 0.15625
- w_down: bfloat16 [6144, 1536], P('mlp'), may hold values from -0.078125 to 0.078125
- w_head: bfloat16 [1536, 64], replicated, may hold values from -0.078125 to 0.078125
Outputs:
- velocity: float32 [256, 8, 64], P(('seq', 'mlp'), 'cfg')
- next_latent: float32 [256, 8, 64], P(('seq', 'mlp'), 'cfg')
- denoised: float32 [256, 8, 64], P(('seq', 'mlp'), 'cfg')
The draws below stay inside these ranges and needn't reach their ends.
Inputs may be any that keep to these rules, and one draw needn't show every extreme that they name: Text position j of prompt b in half c is a real token only if j < text_lengths[c, b]; in every draw some length equals 154 and some equals 1.
All inputs are finite; a program needn't handle non-finite values.
Results may differ from the reference program's by a relative error of at most 0.0085.
Values may be sent and summed in bfloat16 or wider, within the bound.
A program may use at most 128 MiB of HBM per device.

```python
import math
import jax
import jax.numpy as jnp
from jax import lax

D = 1536
HEADS = 24
HEAD_DIM = 64
MLP_UNITS = 6144
PATCH_CH = 64
PROMPTS = 8
TXT = 154
STEPS = 28
IMG = 256
N_MLP = 2


def draw_text_lengths(key, part):
    first, second, third = jax.random.split(key, 3)
    count = 2 * PROMPTS
    values = jax.random.randint(first, (count,), 1, TXT + 1)
    top_slot = jax.random.randint(second, (), 0, count)
    low_slot = (top_slot + 1 + jax.random.randint(third, (), 0, count - 1)) % count
    values = values.at[top_slot].set(TXT).at[low_slot].set(1)
    return values.reshape(2, PROMPTS).astype(jnp.int32)


def block_levels(rng, shape, pieces, least, high):
    level = 1.0
    for axis_at, parts in pieces:
        draws = jax.random.uniform(jax.random.fold_in(jax.random.fold_in(rng, 6), axis_at), (parts,), jnp.float32, least / len(pieces), high / len(pieces))
        level = level * jnp.repeat(jnp.exp(draws), shape[axis_at] // parts).reshape((-1,) + (1,) * (len(shape) - 1 - axis_at))
    return level


def gaussian(stream_key, shape, scale, most, pieces=(), held_as=jnp.bfloat16):
    result = scale * jax.random.normal(stream_key, shape, jnp.float32)
    if pieces:
        result = result * block_levels(stream_key, shape, pieces, -0.22, 0.18)
    return jnp.clip(result, -most, most).astype(held_as)


def setup_inputs(seed: int = 0) -> dict:
    key_of = jax.random.split(jax.random.key(seed), 14)
    image_hidden = gaussian(key_of[0], (2, IMG, PROMPTS, D), 1.0, 6.0, ((0, 2), (1, 16)))
    text_hidden = gaussian(key_of[1], (2, PROMPTS * TXT, D), 1.0, 6.0, ((0, 2), (1, 8)))
    modulation = gaussian(key_of[2], (2, PROMPTS, 10, D), 0.5, 3.0, ((0, 2),), jnp.float32)
    text_lengths = draw_text_lengths(jax.random.fold_in(key_of[13], 71), 0)
    timestep = jax.random.randint(key_of[4], (1,), 0, STEPS).astype(jnp.int32)
    latent = gaussian(key_of[5], (IMG, PROMPTS, PATCH_CH), 1.0, 6.0, ((0, 16), (1, 2)), jnp.float32)
    w_qkv = gaussian(key_of[6], (3, D, D), D ** -0.5, 0.15625, ((2, 2),))
    w_out = gaussian(key_of[7], (D, D), D ** -0.5, 0.15625, ((0, 2),))
    w_text_kv = gaussian(key_of[8], (2, D, D), D ** -0.5, 0.15625, ((2, 2),))
    norm_gain = jnp.clip(jnp.exp(jax.random.uniform(key_of[9], (3, HEAD_DIM), jnp.float32, math.log(1.0), math.log(2.0))), 1.0, 2.0)
    w_up = gaussian(key_of[10], (D, MLP_UNITS), D ** -0.5, 0.15625, ((1, 2),))
    w_down = gaussian(key_of[11], (MLP_UNITS, D), MLP_UNITS ** -0.5, 0.078125, ((0, 2),))
    w_head = gaussian(key_of[12], (D, PATCH_CH), (4 * D) ** -0.5, 0.078125)
    return {"image_hidden": image_hidden, "text_hidden": text_hidden, "modulation": modulation, "text_lengths": text_lengths, "timestep": timestep, "latent": latent, "w_qkv": w_qkv, "w_out": w_out, "w_text_kv": w_text_kv, "norm_gain": norm_gain, "w_up": w_up, "w_down": w_down, "w_head": w_head}


EPS = 1e-06
GUIDE = 4.5
SHIFT = 3.0

def layer_norm(values):
    mean = lax.optimization_barrier(jnp.mean(values, axis=-1, keepdims=True))
    centred = values - mean
    spread = lax.optimization_barrier(jnp.mean(centred * centred, axis=-1, keepdims=True))
    return centred * lax.rsqrt(spread + EPS)

def modulate(values, shift, scale):
    return layer_norm(values) * (1.0 + scale) + shift

def head_norm(values, gain):
    shaped = values.reshape(values.shape[:-1] + (values.shape[-1] // HEAD_DIM, HEAD_DIM))
    square = lax.optimization_barrier(jnp.mean(shaped * shaped, axis=-1, keepdims=True))
    return (shaped * lax.rsqrt(square + EPS) * gain).astype(jnp.bfloat16)

def grouped_sum(inputs, weight, groups):
    width = inputs.shape[1] // groups

    def add_group(total, group):
        part_in = lax.dynamic_slice_in_dim(inputs, group * width, width, 1)
        part_w = lax.dynamic_slice_in_dim(weight, group * width, width, 0)
        term = jnp.dot(part_in, part_w, preferred_element_type=jnp.float32).astype(jnp.bfloat16)
        term = lax.optimization_barrier(term)
        return (total + term.astype(jnp.float32), None)
    start = jnp.zeros((inputs.shape[0], weight.shape[1]), jnp.float32)
    return lax.scan(add_group, start, jnp.arange(groups, dtype=jnp.int32))[0]

def sigma_of(index):
    level = 1.0 - index.astype(jnp.float32) / STEPS
    return SHIFT * level / (1.0 + (SHIFT - 1.0) * level)

def attend(items):
    query, key_img, value_img, key_txt, value_txt, keep = items
    factor = 1.0 / math.sqrt(HEAD_DIM)
    query_f = query.astype(jnp.float32)
    score_img = jnp.einsum('qhd,khd->hqk', query_f, key_img.astype(jnp.float32)) * factor
    score_txt = jnp.einsum('qhd,khd->hqk', query_f, key_txt.astype(jnp.float32)) * factor
    weight_img = jnp.exp(score_img)
    weight_txt = jnp.exp(score_txt) * keep[None, None, :]
    round_img = lax.optimization_barrier(weight_img.astype(jnp.bfloat16))
    round_txt = lax.optimization_barrier(weight_txt.astype(jnp.bfloat16))
    numer = jnp.einsum('hqk,khd->qhd', round_img.astype(jnp.float32), value_img.astype(jnp.float32))
    numer = numer + jnp.einsum('hqk,khd->qhd', round_txt.astype(jnp.float32), value_txt.astype(jnp.float32))
    denom = lax.optimization_barrier(jnp.sum(weight_img, axis=-1)) + lax.optimization_barrier(jnp.sum(weight_txt, axis=-1))
    return (numer / jnp.transpose(denom)[:, :, None]).astype(jnp.bfloat16)

def half_velocity(hidden, text, mods, lengths, w_qkv, w_out, w_text_kv, norm_gain, w_up, w_down, w_head):
    total_rows = IMG * PROMPTS
    hid = hidden.astype(jnp.float32)
    normed = modulate(hid, mods[:, 0], mods[:, 1]).astype(jnp.bfloat16).reshape(total_rows, D)
    query = head_norm(jnp.dot(normed, w_qkv[0], preferred_element_type=jnp.float32), norm_gain[0])
    query = query.reshape(IMG, PROMPTS, HEADS, HEAD_DIM)
    keys = head_norm(jnp.dot(normed, w_qkv[1], preferred_element_type=jnp.float32), norm_gain[1])
    keys = keys.reshape(IMG, PROMPTS, HEADS, HEAD_DIM)
    values = jnp.dot(normed, w_qkv[2], preferred_element_type=jnp.float32).astype(jnp.bfloat16)
    values = values.reshape(IMG, PROMPTS, HEADS, HEAD_DIM)
    text_f = text.astype(jnp.float32).reshape(PROMPTS, TXT, D)
    text_normed = modulate(text_f, mods[:, 6][:, None], mods[:, 7][:, None]).astype(jnp.bfloat16)
    text_normed = text_normed.reshape(PROMPTS * TXT, D)
    text_keys = head_norm(jnp.dot(text_normed, w_text_kv[0], preferred_element_type=jnp.float32), norm_gain[2])
    text_keys = text_keys.reshape(PROMPTS, TXT, HEADS, HEAD_DIM)
    text_values = jnp.dot(text_normed, w_text_kv[1], preferred_element_type=jnp.float32).astype(jnp.bfloat16)
    text_values = text_values.reshape(PROMPTS, TXT, HEADS, HEAD_DIM)
    keep = (jnp.arange(TXT, dtype=jnp.int32)[None, :] < lengths[:, None]).astype(jnp.float32)
    attended = lax.map(attend, (jnp.transpose(query, (1, 0, 2, 3)), jnp.transpose(keys, (1, 0, 2, 3)), jnp.transpose(values, (1, 0, 2, 3)), text_keys, text_values, keep))
    attended = jnp.transpose(attended, (1, 0, 2, 3)).reshape(total_rows, D)
    attention_out = grouped_sum(attended, w_out, N_MLP).reshape(IMG, PROMPTS, D)
    first = hid + mods[:, 2] * attention_out
    mlp_in = modulate(first, mods[:, 3], mods[:, 4]).astype(jnp.bfloat16).reshape(total_rows, D)
    raised = jnp.dot(mlp_in, w_up, preferred_element_type=jnp.float32)
    activated = jax.nn.gelu(raised, approximate=True).astype(jnp.bfloat16)
    mlp_out = grouped_sum(activated, w_down, N_MLP).reshape(IMG, PROMPTS, D)
    second = first + mods[:, 5] * mlp_out
    final = modulate(second, mods[:, 8], mods[:, 9]).astype(jnp.bfloat16).reshape(total_rows, D)
    return jnp.dot(final, w_head, preferred_element_type=jnp.float32).reshape(IMG, PROMPTS, PATCH_CH)

def reference(image_hidden, text_hidden, modulation, text_lengths, timestep, latent, w_qkv, w_out, w_text_kv, norm_gain, w_up, w_down, w_head):
    halves = []
    for branch in range(2):
        halves.append(half_velocity(image_hidden[branch], text_hidden[branch], modulation[branch], text_lengths[branch], w_qkv, w_out, w_text_kv, norm_gain, w_up, w_down, w_head))
    velocity = halves[1] + GUIDE * (halves[0] - halves[1])
    sigma_now = sigma_of(timestep[0])
    sigma_after = sigma_of(timestep[0] + 1)
    next_latent = latent + (sigma_after - sigma_now) * velocity
    denoised = latent - sigma_now * velocity
    return (velocity, next_latent, denoised)
```

```python
import math

import jax
import jax.numpy as jnp
from jax import lax
from jax.experimental import pallas as pl
from jax.experimental.pallas import tpu as pltpu
from jax.sharding import PartitionSpec as P

HEAD_DIM = 64
TXT = 154
STEPS = 28


EPS = 1e-06
GUIDE = 4.5
SHIFT = 3.0
PROMPTS = 8
PATCH = 64
MESH = pl.DeviceIdType.MESH


def partner_2(block, axis, stride):
    count = lax.axis_size(axis)
    route = []
    for low in range(count):
        high = low | 1 << stride
        if high != low and high < count:
            route += [(low, high), (high, low)]
    return lax.ppermute(block, axis, route)


def layer_norm(values):
    mean = jnp.mean(values, axis=-1, keepdims=True)
    centred = values - mean
    spread = jnp.mean(centred * centred, axis=-1, keepdims=True)
    return centred * lax.rsqrt(spread + EPS)


def modulate(values, shift, scale):
    return layer_norm(values) * (1.0 + scale) + shift


def head_norm(values, gain):
    shaped = values.reshape(values.shape[:-1] + (values.shape[-1] // HEAD_DIM, HEAD_DIM))
    square = jnp.mean(shaped * shaped, axis=-1, keepdims=True)
    return (shaped * lax.rsqrt(square + EPS) * gain).astype(jnp.bfloat16)


def sigma_of(index):
    level = 1.0 - index.astype(jnp.float32) / STEPS
    return SHIFT * level / (1.0 + (SHIFT - 1.0) * level)


def project_image(normed_rows, w_qkv, norm_gain):
    query = head_norm(
        jnp.einsum("tbd,de->tbe", normed_rows, w_qkv[0], preferred_element_type=jnp.float32),
        norm_gain[0],
    )
    keys = head_norm(
        jnp.einsum("tbd,de->tbe", normed_rows, w_qkv[1], preferred_element_type=jnp.float32),
        norm_gain[1],
    )
    values = jnp.einsum(
        "tbd,de->tbe", normed_rows, w_qkv[2], preferred_element_type=jnp.float32
    ).astype(jnp.bfloat16)
    flat_query = query.reshape(query.shape[:-2] + (-1,))
    flat_keys = keys.reshape(keys.shape[:-2] + (-1,))
    return jnp.concatenate([flat_query, flat_keys, values], axis=-1)


def key_terms(query, key_rows, value_rows, keep):
    factor = 1.0 / math.sqrt(HEAD_DIM)
    prompts = query.shape[1]
    if keep is None:
        keep = jnp.ones((prompts, key_rows.shape[0]), jnp.float32)

    def one_prompt(items):
        query_rows, keys_one, values_one, keep_one = items
        scores = (
            jnp.einsum("qhd,khd->hqk", query_rows, keys_one, preferred_element_type=jnp.float32)
            * factor
        )
        weights = jnp.exp(scores) * keep_one[None, None, :]
        numer = jnp.einsum(
            "hqk,khd->hqd",
            weights.astype(jnp.bfloat16),
            values_one,
            preferred_element_type=jnp.float32,
        )
        return (numer, jnp.sum(weights, axis=-1))

    return lax.map(
        one_prompt,
        (
            jnp.moveaxis(query, 1, 0),
            jnp.moveaxis(key_rows, 1, 0),
            jnp.moveaxis(value_rows, 1, 0),
            keep,
        ),
    )


def shards(
    image_hidden,
    text_hidden,
    modulation,
    text_lengths,
    timestep,
    latent,
    w_qkv,
    w_out,
    w_text_kv,
    norm_gain,
    w_up,
    w_down,
    w_head,
):
    mods = modulation[0]
    own_hidden = image_hidden[0]
    rows = own_hidden.shape[0]
    width = w_out.shape[0]
    heads = width // HEAD_DIM
    prompts = mods.shape[0]
    offset = lax.axis_index("mlp") * rows
    block_hidden = lax.all_gather(own_hidden, "mlp", axis=0, tiled=True).astype(jnp.float32)
    normed = modulate(block_hidden, mods[:, 0], mods[:, 1]).astype(jnp.bfloat16)
    projected = project_image(normed, w_qkv, norm_gain)
    block_rows = projected.shape[0]
    query = projected[..., :width].reshape(block_rows, prompts, heads, HEAD_DIM)
    own_pairs = projected[..., width:]
    text_rows = text_hidden.shape[1]
    position = lax.axis_index("seq") * text_rows + lax.iota(jnp.int32, text_rows)
    owner = position // TXT
    pick = (owner[:, None] == lax.iota(jnp.int32, prompts)[None, :]).astype(jnp.float32)
    text_shift = jnp.dot(pick, mods[:, 6], precision=lax.Precision.HIGHEST)
    text_scale = jnp.dot(pick, mods[:, 7], precision=lax.Precision.HIGHEST)
    text_normed = modulate(text_hidden[0].astype(jnp.float32), text_shift, text_scale).astype(
        jnp.bfloat16
    )
    text_keys = head_norm(
        jnp.dot(text_normed, w_text_kv[0], preferred_element_type=jnp.float32), norm_gain[2]
    )
    text_keys = text_keys.reshape(text_rows, width)
    text_values = jnp.dot(text_normed, w_text_kv[1], preferred_element_type=jnp.float32).astype(
        jnp.bfloat16
    )
    text_pairs = jnp.concatenate([text_keys, text_values], axis=-1)
    keep = (lax.iota(jnp.int32, TXT)[None, :] < text_lengths[0][:, None]).astype(jnp.float32)

    def split_pairs(pairs):
        shape = pairs.shape[:2] + (heads, HEAD_DIM)
        return (pairs[..., :width].reshape(shape), pairs[..., width:].reshape(shape))

    all_image, all_text = (
        lax.all_gather(own_pairs, "seq", axis=0, tiled=True),
        lax.all_gather(text_pairs, "seq", axis=0, tiled=True),
    )
    shaped = jnp.transpose(all_text.reshape(prompts, TXT, 2 * width), (1, 0, 2))
    key_rows, value_rows = split_pairs(shaped)
    text_numer, text_denom = key_terms(query, key_rows, value_rows, keep)
    key_rows, value_rows = split_pairs(all_image)
    image_numer, image_denom = key_terms(query, key_rows, value_rows, None)
    numer = text_numer + image_numer
    denom = text_denom + image_denom
    attended = (numer / denom[..., None]).astype(jnp.bfloat16)
    attended = jnp.transpose(attended, (2, 0, 1, 3)).reshape(block_rows, prompts, width)
    part = attended
    attention_out = lax.psum(
        jnp.einsum("tbe,ed->tbd", part, w_out, preferred_element_type=jnp.float32).astype(
            jnp.bfloat16
        ),
        "mlp",
    ).astype(jnp.float32)
    first = block_hidden + mods[:, 2] * attention_out
    mlp_in = modulate(first, mods[:, 3], mods[:, 4]).astype(jnp.bfloat16)
    raised = jnp.einsum("tbd,du->tbu", mlp_in, w_up, preferred_element_type=jnp.float32)
    activated = jax.nn.gelu(raised, approximate=True).astype(jnp.bfloat16)
    own_first = lax.dynamic_slice_in_dim(first, offset, rows, 0)
    part = activated
    mlp_out = lax.psum_scatter(
        jnp.einsum("tbu,ud->tbd", part, w_down, preferred_element_type=jnp.float32).astype(
            jnp.bfloat16
        ),
        "mlp",
        scatter_dimension=0,
        tiled=True,
    ).astype(jnp.float32)
    second = own_first + mods[:, 5] * mlp_out
    final = modulate(second, mods[:, 8], mods[:, 9]).astype(jnp.bfloat16)
    own_velocity = jnp.einsum("tbd,dp->tbp", final, w_head, preferred_element_type=jnp.float32)
    half_count = prompts // 2
    branch = lax.axis_index("cfg")
    outgoing = lax.dynamic_slice_in_dim(own_velocity, (1 - branch) * half_count, half_count, 1)
    kept = lax.dynamic_slice_in_dim(own_velocity, branch * half_count, half_count, 1)
    partner = partner_2(outgoing, "cfg", 0)
    is_conditional = branch == 0
    conditional = jnp.where(is_conditional, kept, partner)
    unconditional = jnp.where(is_conditional, partner, kept)
    velocity = unconditional + GUIDE * (conditional - unconditional)
    sigma_now = sigma_of(timestep[0])
    sigma_after = sigma_of(timestep[0] + 1)
    next_latent = latent + (sigma_after - sigma_now) * velocity
    denoised = latent - sigma_now * velocity
    return (velocity, next_latent, denoised)

def fused_kernel(
    hid_ref, text_ref, mod_ref, len_ref, step_ref, latent_ref, wqkv_hbm, wout_hbm, wtext_hbm,
    gain_ref, wup_hbm, wdown_hbm, whead_ref,
    vel_ref, next_ref, den_ref,
    wqkv, wout, wtext, wup, wdown,
    wide, ready, gathered, normed, text_norm, q6, k6, v6, kt6, vt6, attended,
    part, part_in, first_buf, mlp_in, act, down, down_in, final, half_out, half_in,
    wsem, a2a_send, a2a_recv, fwd_send, fwd_recv, rs_send, rs_recv, ag_send, ag_recv,
    dn_send, dn_recv, out_send, out_recv,
):
    c = lax.axis_index("cfg")
    s = lax.axis_index("seq")
    m = lax.axis_index("mlp")
    other = 1 - m
    ring = PROMPTS
    rows = hid_ref.shape[0]
    own_rows = rows * ring
    width = wout.shape[0]
    model = wout.shape[1]
    units = wup.shape[1]
    pairs = width // 128
    txt_pad = text_norm.shape[0]
    txt = text_ref.shape[0]
    f32, bf16 = jnp.float32, jnp.bfloat16
    partner = (c, s, other)

    loads = []
    jobs = [(wtext_hbm.at[i], wtext.at[i]) for i in range(2)]
    jobs += [(wqkv_hbm.at[i], wqkv.at[i]) for i in range(3)]
    jobs += [(wout_hbm, wout)]
    jobs += [(wup_hbm.at[pl.ds(i * model // 2, model // 2)], wup.at[pl.ds(i * model // 2, model // 2)]) for i in range(2)]
    jobs += [(wdown_hbm.at[pl.ds(i * units // 2, units // 2)], wdown.at[pl.ds(i * units // 2, units // 2)]) for i in range(2)]
    for i, (src, dst) in enumerate(jobs):
        loads.append(pltpu.make_async_copy(src, dst, wsem.at[i]))
        loads[-1].start()

    barrier = pltpu.get_barrier_semaphore()
    for k in range(ring):
        dest = lax.rem(s + k, ring)
        if k:
            pl.semaphore_signal(barrier, inc=1, device_id=(c, dest, m), device_id_type=MESH)
        pl.semaphore_signal(barrier, inc=1, device_id=(1 - c, dest, m), device_id_type=MESH)
    pl.semaphore_signal(barrier, inc=1, device_id=partner, device_id_type=MESH)

    lanes = model // 128
    for j in range(lanes):
        tile = hid_ref[:, :, j * 128 : (j + 1) * 128]
        wide[j] = tile.astype(f32).reshape(own_rows, 128)
    for p in range(ring):
        for j in range(lanes):
            ready[p, :, j * 128 : (j + 1) * 128] = wide[j, pl.ds(p, rows, stride=ring), :].astype(bf16)
    gathered[m, s] = ready[s]
    pl.semaphore_wait(barrier, 2 * ring)

    sends = []
    a2a = []
    for k in range(1, ring):
        dest = lax.rem(s + k, ring)
        cp = pltpu.make_async_remote_copy(
            src_ref=ready.at[dest], dst_ref=gathered.at[m, s],
            send_sem=a2a_send.at[k], recv_sem=a2a_recv.at[k],
            device_id=(c, dest, m), device_id_type=MESH)
        cp.start()
        sends.append(cp)

    def forward(k):
        src = lax.rem(s + ring - k, ring)
        if k:
            pltpu.make_async_remote_copy(
                src_ref=ready.at[src], dst_ref=gathered.at[m, src],
                send_sem=a2a_send.at[k], recv_sem=a2a_recv.at[k],
                device_id=(c, src, m), device_id_type=MESH).wait_recv()
        cp = pltpu.make_async_remote_copy(
            src_ref=gathered.at[m, src], dst_ref=gathered.at[m, src],
            send_sem=fwd_send.at[k], recv_sem=fwd_recv.at[k],
            device_id=partner, device_id_type=MESH)
        cp.start()
        sends.append(cp)

    forward(0)

    def mod_row(k):
        return mod_ref[k, pl.ds(s, 1), :]

    def norm_rows(values, k):
        mean = jnp.mean(values, axis=-1, keepdims=True)
        centred = values - mean
        spread = jnp.mean(centred * centred, axis=-1, keepdims=True)
        return centred * lax.rsqrt(spread + EPS) * (1.0 + mod_row(k + 1)) + mod_row(k)

    whole_blocks = txt // 16

    def text_block(i, carry):
        at = pl.ds(pl.multiple_of(i * 16, 16), 16)
        text_norm[at, :] = norm_rows(text_ref[at, :].astype(f32), 6)
        return carry

    lax.fori_loop(0, whole_blocks, text_block, 0)
    tail = txt - whole_blocks * 16
    if tail:
        text_norm[whole_blocks * 16 : txt, :] = norm_rows(
            text_ref[whole_blocks * 16 : txt, :].astype(f32), 6)
    if txt_pad > txt:
        text_norm[txt:txt_pad, :] = jnp.zeros((txt_pad - txt, model), f32)

    forward(1)
    forward(2)

    row_id = lax.broadcasted_iota(jnp.int32, (2 * 128, 128), 0)
    col_id = lax.broadcasted_iota(jnp.int32, (2 * 128, 128), 1)
    same_head = (((row_id // HEAD_DIM) % 2) == (col_id // HEAD_DIM)).astype(f32).astype(bf16)

    def head_norm_tile(u, gain):
        square = u * u
        high = square.astype(bf16)
        low = (square - high.astype(f32)).astype(bf16)
        total = jnp.dot(jnp.concatenate([high, low], axis=1), same_head, preferred_element_type=f32)
        return (u * lax.rsqrt(total * (1.0 / HEAD_DIM) + EPS) * gain).astype(bf16)

    def gain_of(i):
        one = gain_ref[i : i + 1, :]
        return jnp.concatenate([one, one], axis=1)

    keep = (lax.broadcasted_iota(jnp.int32, (txt_pad, 128), 0) < len_ref[0, s]).astype(f32).astype(bf16)
    lane = lax.broadcasted_iota(jnp.int32, (1, 128), 1)
    low_lane = (lane < HEAD_DIM).astype(f32).astype(bf16)
    high_lane = (lane >= HEAD_DIM).astype(f32).astype(bf16)

    def project(lhs, weight, out6, gain, mask):
        def chunk(j, carry):
            at = pl.ds(pl.multiple_of(j * 256, 256), 256)
            u = jnp.dot(lhs, weight[:, at], preferred_element_type=f32)
            for t in range(2):
                tile = u[:, t * 128 : (t + 1) * 128]
                if gain is None:
                    res = tile.astype(bf16)
                else:
                    res = head_norm_tile(tile, gain)
                if mask is not None:
                    res = res * mask
                out6[2 * j + t] = res
            return carry

        lax.fori_loop(0, width // 256, chunk, 0)

    text_lhs = text_norm[...].astype(bf16)
    loads[0].wait()
    project(text_lhs, wtext.at[0], kt6, gain_of(2), None)
    forward(3)
    forward(4)
    loads[1].wait()
    project(text_lhs, wtext.at[1], vt6, None, keep)
    for k in range(5, ring):
        forward(k)

    def norm_half(half):
        def block(i, carry):
            normed[half, i] = norm_rows(gathered[half, i].astype(f32), 0).astype(bf16)
            return carry

        lax.fori_loop(0, ring, block, 0)

    norm_half(m)
    for k in range(ring):
        src = lax.rem(s + ring - k, ring)
        pltpu.make_async_remote_copy(
            src_ref=gathered.at[other, src], dst_ref=gathered.at[other, src],
            send_sem=fwd_send.at[k], recv_sem=fwd_recv.at[k],
            device_id=partner, device_id_type=MESH).wait_recv()
    norm_half(other)

    image_lhs = normed[...].reshape(2 * own_rows, model)
    loads[2].wait()
    project(image_lhs, wqkv.at[0], q6, gain_of(0) * (1.0 / math.sqrt(HEAD_DIM)), None)
    loads[3].wait()
    project(image_lhs, wqkv.at[1], k6, gain_of(1), None)
    loads[4].wait()
    project(image_lhs, wqkv.at[2], v6, None, None)

    def dot_t(a, b):
        return lax.dot_general(a, b, (((1,), (1,)), ((), ())), preferred_element_type=f32)

    def pair(p, carry):
        q, k, v, kt, vt = q6[p], k6[p], v6[p], kt6[p], vt6[p]
        outs = []
        for mine, rest in ((low_lane, high_lane), (high_lane, low_lane)):
            qh = q * mine
            w_img = jnp.exp(dot_t(qh, k)).astype(bf16)
            w_txt = jnp.exp(dot_t(qh, kt)).astype(bf16)
            outs.append(
                jnp.dot(w_img, v * mine + rest, preferred_element_type=f32)
                + jnp.dot(w_txt, vt * mine + keep * rest, preferred_element_type=f32))
        numer = jnp.where(lane < HEAD_DIM, outs[0], outs[1])
        denom = pltpu.roll(jnp.where(lane < HEAD_DIM, outs[1], outs[0]), HEAD_DIM, 1)
        attended[:, pl.ds(pl.multiple_of(p * 128, 128), 128)] = (numer / denom).astype(bf16)
        return carry

    lax.fori_loop(0, pairs, pair, 0)

    chunks = part_in.shape[0]
    span = model // chunks
    loads[5].wait()
    att = attended[...]
    for j in range(chunks):
        res = jnp.dot(att, wout[:, j * span : (j + 1) * span], preferred_element_type=f32).astype(bf16)
        part[0, j] = res[:own_rows].reshape(ring, rows, span)
        part[1, j] = res[own_rows:].reshape(ring, rows, span)
        cp = pltpu.make_async_remote_copy(
            src_ref=part.at[other, j], dst_ref=part_in.at[j],
            send_sem=rs_send.at[j], recv_sem=rs_recv.at[j],
            device_id=partner, device_id_type=MESH)
        cp.start()
        sends.append(cp)
    for cp in sends[-chunks:]:
        cp.wait_recv()

    def first_block(i, carry):
        total = jnp.concatenate(
            [part[m, j, i].astype(f32) + part_in[j, i].astype(f32) for j in range(chunks)], axis=1)
        first = gathered[m, i].astype(f32) + mod_row(2) * total
        first_buf[i] = first
        mlp_in[m, i] = norm_rows(first, 3).astype(bf16)
        return carry

    ag = []
    for h in range(2):
        at = pl.ds(h * ring // 2, ring // 2)
        lax.fori_loop(h * ring // 2, (h + 1) * ring // 2, first_block, 0)
        cp = pltpu.make_async_remote_copy(
            src_ref=mlp_in.at[m, at], dst_ref=mlp_in.at[m, at],
            send_sem=ag_send.at[h], recv_sem=ag_recv.at[h],
            device_id=partner, device_id_type=MESH)
        cp.start()
        sends.append(cp)
        ag.append(cp)

    def up(half):
        lhs = mlp_in[half].reshape(own_rows, model)

        def chunk(j, carry):
            at = pl.ds(pl.multiple_of(j * 512, 512), 512)
            r = jnp.dot(lhs, wup[:, at], preferred_element_type=f32)
            inner = math.sqrt(2.0 / math.pi) * (r + 0.044715 * (r * r * r))
            act[half, :, at] = (0.5 * r * (1.0 + jnp.tanh(inner))).astype(bf16)
            return carry

        lax.fori_loop(0, units // 512, chunk, 0)

    loads[6].wait()
    loads[7].wait()
    up(m)
    for cp in ag:
        cp.wait_recv()
    up(other)
    loads[8].wait()
    loads[9].wait()

    dn = []
    for half in (other, m):
        lhs = act[half]
        for j in range(chunks):
            res = jnp.dot(lhs, wdown[:, j * span : (j + 1) * span], preferred_element_type=f32)
            down[half, j] = res.astype(bf16).reshape(ring, rows, span)
            if len(dn) < chunks:
                cp = pltpu.make_async_remote_copy(
                    src_ref=down.at[other, j], dst_ref=down_in.at[j],
                    send_sem=dn_send.at[j], recv_sem=dn_recv.at[j],
                    device_id=partner, device_id_type=MESH)
                cp.start()
                sends.append(cp)
                dn.append(cp)
    for cp in dn:
        cp.wait_recv()

    def final_block(i, carry):
        total = jnp.concatenate(
            [down[m, j, i].astype(f32) + down_in[j, i].astype(f32) for j in range(chunks)], axis=1)
        second = first_buf[i] + mod_row(5) * total
        final[i] = norm_rows(second, 8).astype(bf16)
        return carry

    lax.fori_loop(0, ring, final_block, 0)
    head = whead_ref[...]
    hv = dot_t(final[...].reshape(own_rows, model), jnp.concatenate([head, head], axis=0))
    half_out[...] = hv.reshape(ring, rows, 128)

    home = s // (ring // 2)
    slot = c * (ring // 2) + lax.rem(s, ring // 2)
    at_home = c == home
    for k in range(ring):
        dest = lax.rem(s + k, ring)
        cp = pltpu.make_async_remote_copy(
            src_ref=half_out.at[dest], dst_ref=half_in.at[slot],
            send_sem=out_send.at[k], recv_sem=out_recv.at[slot],
            device_id=(home, dest, m), device_id_type=MESH)
        if k:
            cp.start()
        else:
            own = cp

            @pl.when(at_home)
            def _():
                half_in[slot] = half_out[s]

            @pl.when(jnp.logical_not(at_home))
            def _():
                own.start()

        if k:
            sends.append(cp)
    for q in range(ring):
        branch, local = q // (ring // 2), q % (ring // 2)
        prompt = c * (ring // 2) + local
        is_self = jnp.logical_and(c == branch, s == prompt)

        @pl.when(jnp.logical_not(is_self))
        def _():
            pltpu.make_async_remote_copy(
                src_ref=half_out.at[0], dst_ref=half_in.at[q],
                send_sem=out_send.at[0], recv_sem=out_recv.at[q],
                device_id=(branch, prompt, m), device_id_type=MESH).wait_recv()

    t = step_ref[0]

    def sigma(index):
        level = 1.0 - jnp.full((1, PATCH), index, jnp.int32).astype(f32) / STEPS
        return SHIFT * level / (1.0 + (SHIFT - 1.0) * level)

    now, after = sigma(t), sigma(t + 1)
    for p in range(ring // 2):
        cond = half_in[p][:, :PATCH]
        uncond = half_in[ring // 2 + p][:, :PATCH]
        velocity = uncond + GUIDE * (cond - uncond)
        base = latent_ref[:, p, :]
        vel_ref[:, p, :] = velocity
        next_ref[:, p, :] = base + (after - now) * velocity
        den_ref[:, p, :] = base - now * velocity

    for cp in sends:
        cp.wait_send()

    @pl.when(jnp.logical_not(at_home))
    def _():
        own.wait_send()


def fused_shards(
    image_hidden, text_hidden, modulation, text_lengths, timestep, latent,
    w_qkv, w_out, w_text_kv, norm_gain, w_up, w_down, w_head,
):
    f32, bf16 = jnp.float32, jnp.bfloat16
    rows, prompts, model = image_hidden.shape[1:]
    txt = text_hidden.shape[1]
    txt_pad = -(-txt // 16) * 16
    width = w_out.shape[0]
    units = w_up.shape[1]
    own_rows = rows * prompts
    pairs = width // 128
    chunks = 3
    span = model // chunks
    vmem = pl.BlockSpec(memory_space=pltpu.VMEM)
    smem = pl.BlockSpec(memory_space=pltpu.SMEM)
    anym = pl.BlockSpec(memory_space=pl.ANY)
    dma = pltpu.SemaphoreType.DMA
    out = jax.ShapeDtypeStruct(latent.shape, f32)
    scratch = [
        pltpu.VMEM(w_qkv.shape, bf16), pltpu.VMEM(w_out.shape, bf16), pltpu.VMEM(w_text_kv.shape, bf16),
        pltpu.VMEM(w_up.shape, bf16), pltpu.VMEM(w_down.shape, bf16),
        pltpu.VMEM((model // 128, own_rows, 128), f32),
        pltpu.VMEM((prompts, rows, model), bf16),
        pltpu.VMEM((2, prompts, rows, model), bf16),
        pltpu.VMEM((2, prompts, rows, model), bf16),
        pltpu.VMEM((txt_pad, model), f32),
        pltpu.VMEM((pairs, 2 * own_rows, 128), bf16),
        pltpu.VMEM((pairs, 2 * own_rows, 128), bf16),
        pltpu.VMEM((pairs, 2 * own_rows, 128), bf16),
        pltpu.VMEM((pairs, txt_pad, 128), bf16),
        pltpu.VMEM((pairs, txt_pad, 128), bf16),
        pltpu.VMEM((2 * own_rows, width), bf16),
        pltpu.VMEM((2, chunks, prompts, rows, span), bf16),
        pltpu.VMEM((chunks, prompts, rows, span), bf16),
        pltpu.VMEM((prompts, rows, model), f32),
        pltpu.VMEM((2, prompts, rows, model), bf16),
        pltpu.VMEM((2, own_rows, units), bf16),
        pltpu.VMEM((2, chunks, prompts, rows, span), bf16),
        pltpu.VMEM((chunks, prompts, rows, span), bf16),
        pltpu.VMEM((prompts, rows, model), bf16),
        pltpu.VMEM((prompts, rows, 128), f32),
        pltpu.VMEM((prompts, rows, 128), f32),
        dma((10,)), dma((prompts,)), dma((prompts,)), dma((prompts,)), dma((prompts,)),
        dma((chunks,)), dma((chunks,)), dma((2,)), dma((2,)), dma((chunks,)), dma((chunks,)),
        dma((prompts,)), dma((prompts,)),
    ]
    return pl.pallas_call(
        fused_kernel,
        out_shape=(out, out, out),
        in_specs=[vmem, vmem, vmem, smem, smem, vmem, anym, anym, anym, vmem, anym, anym, vmem],
        out_specs=(vmem, vmem, vmem),
        scratch_shapes=scratch,
        compiler_params=pltpu.CompilerParams(
            collective_id=0, has_side_effects=True, vmem_limit_bytes=60 << 20),
        name="fused_block",
    )(
        image_hidden[0], text_hidden[0], jnp.transpose(modulation[0], (1, 0, 2)), text_lengths,
        timestep, latent, w_qkv, w_out, w_text_kv, norm_gain, w_up, w_down, jnp.transpose(w_head),
    )


def solution(mesh):
    placed = (
        P("cfg", ("seq", "mlp"), None, None),
        P("cfg", "seq", None),
        P("cfg", None, None, None),
        P("cfg", None),
        P(),
        P(("seq", "mlp"), "cfg", None),
        P(None, None, "mlp"),
        P("mlp", None),
        P(None, None, "mlp"),
        P(),
        P(None, "mlp"),
        P("mlp", None),
        P(),
    )
    fits = mesh.shape["cfg"] == 2 and mesh.shape["seq"] == PROMPTS and mesh.shape["mlp"] == 2
    return jax.shard_map(
        fused_shards if fits else shards,
        mesh=mesh,
        in_specs=placed,
        out_specs=(
            P(("seq", "mlp"), "cfg", None),
            P(("seq", "mlp"), "cfg", None),
            P(("seq", "mlp"), "cfg", None),
        ),
        check_vma=False,
    )
```

```python
import math

import jax
import jax.numpy as jnp
from jax import lax
from jax.experimental import pallas as pl
from jax.experimental.pallas import tpu as pltpu
from jax.sharding import PartitionSpec as P

HEAD_DIM = 64
TXT = 154
STEPS = 28


EPS = 1e-06
GUIDE = 4.5
SHIFT = 3.0
PROMPTS = 8
PATCH = 64
MESH = pl.DeviceIdType.MESH


def partner_2(block, axis, stride):
    count = lax.axis_size(axis)
    route = []
    for low in range(count):
        high = low | 1 << stride
        if high != low and high < count:
            route += [(low, high), (high, low)]
    return lax.ppermute(block, axis, route)


def layer_norm(values):
    mean = jnp.mean(values, axis=-1, keepdims=True)
    centred = values - mean
    spread = jnp.mean(centred * centred, axis=-1, keepdims=True)
    return centred * lax.rsqrt(spread + EPS)


def modulate(values, shift, scale):
    return layer_norm(values) * (1.0 + scale) + shift


def head_norm(values, gain):
    shaped = values.reshape(values.shape[:-1] + (values.shape[-1] // HEAD_DIM, HEAD_DIM))
    square = jnp.mean(shaped * shaped, axis=-1, keepdims=True)
    return (shaped * lax.rsqrt(square + EPS) * gain).astype(jnp.bfloat16)


def sigma_of(index):
    level = 1.0 - index.astype(jnp.float32) / STEPS
    return SHIFT * level / (1.0 + (SHIFT - 1.0) * level)


def project_image(normed_rows, w_qkv, norm_gain):
    query = head_norm(
        jnp.einsum("tbd,de->tbe", normed_rows, w_qkv[0], preferred_element_type=jnp.float32),
        norm_gain[0],
    )
    keys = head_norm(
        jnp.einsum("tbd,de->tbe", normed_rows, w_qkv[1], preferred_element_type=jnp.float32),
        norm_gain[1],
    )
    values = jnp.einsum(
        "tbd,de->tbe", normed_rows, w_qkv[2], preferred_element_type=jnp.float32
    ).astype(jnp.bfloat16)
    flat_query = query.reshape(query.shape[:-2] + (-1,))
    flat_keys = keys.reshape(keys.shape[:-2] + (-1,))
    return jnp.concatenate([flat_query, flat_keys, values], axis=-1)


def key_terms(query, key_rows, value_rows, keep):
    factor = 1.0 / math.sqrt(HEAD_DIM)
    prompts = query.shape[1]
    if keep is None:
        keep = jnp.ones((prompts, key_rows.shape[0]), jnp.float32)

    def one_prompt(items):
        query_rows, keys_one, values_one, keep_one = items
        scores = (
            jnp.einsum("qhd,khd->hqk", query_rows, keys_one, preferred_element_type=jnp.float32)
            * factor
        )
        weights = jnp.exp(scores) * keep_one[None, None, :]
        numer = jnp.einsum(
            "hqk,khd->hqd",
            weights.astype(jnp.bfloat16),
            values_one,
            preferred_element_type=jnp.float32,
        )
        return (numer, jnp.sum(weights, axis=-1))

    return lax.map(
        one_prompt,
        (
            jnp.moveaxis(query, 1, 0),
            jnp.moveaxis(key_rows, 1, 0),
            jnp.moveaxis(value_rows, 1, 0),
            keep,
        ),
    )


def shards(
    image_hidden,
    text_hidden,
    modulation,
    text_lengths,
    timestep,
    latent,
    w_qkv,
    w_out,
    w_text_kv,
    norm_gain,
    w_up,
    w_down,
    w_head,
):
    mods = modulation[0]
    own_hidden = image_hidden[0]
    rows = own_hidden.shape[0]
    width = w_out.shape[0]
    heads = width // HEAD_DIM
    prompts = mods.shape[0]
    offset = lax.axis_index("mlp") * rows
    block_hidden = lax.all_gather(own_hidden, "mlp", axis=0, tiled=True).astype(jnp.float32)
    normed = modulate(block_hidden, mods[:, 0], mods[:, 1]).astype(jnp.bfloat16)
    projected = project_image(normed, w_qkv, norm_gain)
    block_rows = projected.shape[0]
    query = projected[..., :width].reshape(block_rows, prompts, heads, HEAD_DIM)
    own_pairs = projected[..., width:]
    text_rows = text_hidden.shape[1]
    position = lax.axis_index("seq") * text_rows + lax.iota(jnp.int32, text_rows)
    owner = position // TXT
    pick = (owner[:, None] == lax.iota(jnp.int32, prompts)[None, :]).astype(jnp.float32)
    text_shift = jnp.dot(pick, mods[:, 6], precision=lax.Precision.HIGHEST)
    text_scale = jnp.dot(pick, mods[:, 7], precision=lax.Precision.HIGHEST)
    text_normed = modulate(text_hidden[0].astype(jnp.float32), text_shift, text_scale).astype(
        jnp.bfloat16
    )
    text_keys = head_norm(
        jnp.dot(text_normed, w_text_kv[0], preferred_element_type=jnp.float32), norm_gain[2]
    )
    text_keys = text_keys.reshape(text_rows, width)
    text_values = jnp.dot(text_normed, w_text_kv[1], preferred_element_type=jnp.float32).astype(
        jnp.bfloat16
    )
    text_pairs = jnp.concatenate([text_keys, text_values], axis=-1)
    keep = (lax.iota(jnp.int32, TXT)[None, :] < text_lengths[0][:, None]).astype(jnp.float32)

    def split_pairs(pairs):
        shape = pairs.shape[:2] + (heads, HEAD_DIM)
        return (pairs[..., :width].reshape(shape), pairs[..., width:].reshape(shape))

    all_image, all_text = (
        lax.all_gather(own_pairs, "seq", axis=0, tiled=True),
        lax.all_gather(text_pairs, "seq", axis=0, tiled=True),
    )
    shaped = jnp.transpose(all_text.reshape(prompts, TXT, 2 * width), (1, 0, 2))
    key_rows, value_rows = split_pairs(shaped)
    text_numer, text_denom = key_terms(query, key_rows, value_rows, keep)
    key_rows, value_rows = split_pairs(all_image)
    image_numer, image_denom = key_terms(query, key_rows, value_rows, None)
    numer = text_numer + image_numer
    denom = text_denom + image_denom
    attended = (numer / denom[..., None]).astype(jnp.bfloat16)
    attended = jnp.transpose(attended, (2, 0, 1, 3)).reshape(block_rows, prompts, width)
    part = attended
    attention_out = lax.psum(
        jnp.einsum("tbe,ed->tbd", part, w_out, preferred_element_type=jnp.float32).astype(
            jnp.bfloat16
        ),
        "mlp",
    ).astype(jnp.float32)
    first = block_hidden + mods[:, 2] * attention_out
    mlp_in = modulate(first, mods[:, 3], mods[:, 4]).astype(jnp.bfloat16)
    raised = jnp.einsum("tbd,du->tbu", mlp_in, w_up, preferred_element_type=jnp.float32)
    activated = jax.nn.gelu(raised, approximate=True).astype(jnp.bfloat16)
    own_first = lax.dynamic_slice_in_dim(first, offset, rows, 0)
    part = activated
    mlp_out = lax.psum_scatter(
        jnp.einsum("tbu,ud->tbd", part, w_down, preferred_element_type=jnp.float32).astype(
            jnp.bfloat16
        ),
        "mlp",
        scatter_dimension=0,
        tiled=True,
    ).astype(jnp.float32)
    second = own_first + mods[:, 5] * mlp_out
    final = modulate(second, mods[:, 8], mods[:, 9]).astype(jnp.bfloat16)
    own_velocity = jnp.einsum("tbd,dp->tbp", final, w_head, preferred_element_type=jnp.float32)
    half_count = prompts // 2
    branch = lax.axis_index("cfg")
    outgoing = lax.dynamic_slice_in_dim(own_velocity, (1 - branch) * half_count, half_count, 1)
    kept = lax.dynamic_slice_in_dim(own_velocity, branch * half_count, half_count, 1)
    partner = partner_2(outgoing, "cfg", 0)
    is_conditional = branch == 0
    conditional = jnp.where(is_conditional, kept, partner)
    unconditional = jnp.where(is_conditional, partner, kept)
    velocity = unconditional + GUIDE * (conditional - unconditional)
    sigma_now = sigma_of(timestep[0])
    sigma_after = sigma_of(timestep[0] + 1)
    next_latent = latent + (sigma_after - sigma_now) * velocity
    denoised = latent - sigma_now * velocity
    return (velocity, next_latent, denoised)

def fused_kernel(
    hid_ref, text_ref, mod_ref, len_ref, step_ref, latent_ref, wqkv_hbm, wout_hbm, wtext_hbm,
    gain_ref, wup_hbm, wdown_hbm, whead_ref,
    out_ref,
    wqkv, wout, wtext, wup, wdown,
    wide, ready, gathered, normed, text_norm, q6, k6, v6, kt6, vt6, attended,
    part, part_in, first_buf, mlp_in, act, down, down_in, final, half_out, half_in,
    wsem, a2a_send, a2a_recv, fwd_send, fwd_recv, rs_send, rs_recv, ag_send, ag_recv,
    dn_send, dn_recv, out_send, out_recv,
):
    c = lax.axis_index("cfg")
    s = lax.axis_index("seq")
    m = lax.axis_index("mlp")
    other = 1 - m
    ring = PROMPTS
    rows = hid_ref.shape[0]
    own_rows = rows * ring
    width = wout.shape[0]
    model = wout.shape[1]
    units = wup.shape[1]
    pairs = width // 128
    txt_pad = text_norm.shape[0]
    txt = text_ref.shape[0]
    f32, bf16 = jnp.float32, jnp.bfloat16
    partner = (c, s, other)

    loads = []
    jobs = [(wtext_hbm.at[i], wtext.at[i]) for i in range(2)]
    jobs += [(wqkv_hbm.at[i], wqkv.at[i]) for i in range(3)]
    jobs += [(wout_hbm, wout)]
    jobs += [(wup_hbm.at[pl.ds(i * model // 2, model // 2)], wup.at[pl.ds(i * model // 2, model // 2)]) for i in range(2)]
    jobs += [(wdown_hbm.at[pl.ds(i * units // 2, units // 2)], wdown.at[pl.ds(i * units // 2, units // 2)]) for i in range(2)]
    for i, (src, dst) in enumerate(jobs):
        loads.append(pltpu.make_async_copy(src, dst, wsem.at[i]))
        loads[-1].start()

    barrier = pltpu.get_barrier_semaphore()
    for k in range(ring):
        dest = lax.rem(s + k, ring)
        if k:
            pl.semaphore_signal(barrier, inc=1, device_id=(c, dest, m), device_id_type=MESH)
        pl.semaphore_signal(barrier, inc=1, device_id=(1 - c, dest, m), device_id_type=MESH)
    pl.semaphore_signal(barrier, inc=1, device_id=partner, device_id_type=MESH)

    lanes = model // 128
    for j in range(lanes):
        tile = hid_ref[:, :, j * 128 : (j + 1) * 128]
        wide[j] = tile.astype(f32).reshape(own_rows, 128)
    for p in range(ring):
        for j in range(lanes):
            ready[p, :, j * 128 : (j + 1) * 128] = wide[j, pl.ds(p, rows, stride=ring), :].astype(bf16)
    gathered[m, s] = ready[s]
    pl.semaphore_wait(barrier, 2 * ring)

    sends = []
    a2a = []
    for k in range(1, ring):
        dest = lax.rem(s + k, ring)
        cp = pltpu.make_async_remote_copy(
            src_ref=ready.at[dest], dst_ref=gathered.at[m, s],
            send_sem=a2a_send.at[k], recv_sem=a2a_recv.at[k],
            device_id=(c, dest, m), device_id_type=MESH)
        cp.start()
        sends.append(cp)

    def forward(k):
        src = lax.rem(s + ring - k, ring)
        if k:
            pltpu.make_async_remote_copy(
                src_ref=ready.at[src], dst_ref=gathered.at[m, src],
                send_sem=a2a_send.at[k], recv_sem=a2a_recv.at[k],
                device_id=(c, src, m), device_id_type=MESH).wait_recv()
        cp = pltpu.make_async_remote_copy(
            src_ref=gathered.at[m, src], dst_ref=gathered.at[m, src],
            send_sem=fwd_send.at[k], recv_sem=fwd_recv.at[k],
            device_id=partner, device_id_type=MESH)
        cp.start()
        sends.append(cp)

    forward(0)

    def mod_row(k):
        return mod_ref[k, pl.ds(s, 1), :]

    def norm_rows(values, k):
        mean = jnp.mean(values, axis=-1, keepdims=True)
        centred = values - mean
        spread = jnp.mean(centred * centred, axis=-1, keepdims=True)
        return centred * lax.rsqrt(spread + EPS) * (1.0 + mod_row(k + 1)) + mod_row(k)

    whole_blocks = txt // 16

    def text_block(i, carry):
        at = pl.ds(pl.multiple_of(i * 16, 16), 16)
        text_norm[at, :] = norm_rows(text_ref[at, :].astype(f32), 6)
        return carry

    lax.fori_loop(0, whole_blocks, text_block, 0, unroll=3 if whole_blocks % 3 == 0 else 1)
    tail = txt - whole_blocks * 16
    if tail:
        text_norm[whole_blocks * 16 : txt, :] = norm_rows(
            text_ref[whole_blocks * 16 : txt, :].astype(f32), 6)
    if txt_pad > txt:
        text_norm[txt:txt_pad, :] = jnp.zeros((txt_pad - txt, model), f32)

    forward(1)
    forward(2)

    row_id = lax.broadcasted_iota(jnp.int32, (2 * 128, 128), 0)
    col_id = lax.broadcasted_iota(jnp.int32, (2 * 128, 128), 1)
    same_head = (((row_id // HEAD_DIM) % 2) == (col_id // HEAD_DIM)).astype(f32).astype(bf16)

    def head_norm_tile(u, gain):
        square = u * u
        high = square.astype(bf16)
        low = (square - high.astype(f32)).astype(bf16)
        total = jnp.dot(jnp.concatenate([high, low], axis=1), same_head, preferred_element_type=f32)
        return (u * lax.rsqrt(total * (1.0 / HEAD_DIM) + EPS) * gain).astype(bf16)

    def gain_of(i):
        one = gain_ref[i : i + 1, :]
        return jnp.concatenate([one, one], axis=1)

    keep = (lax.broadcasted_iota(jnp.int32, (txt_pad, 128), 0) < len_ref[0, s]).astype(f32).astype(bf16)
    lane = lax.broadcasted_iota(jnp.int32, (1, 128), 1)
    low_lane = (lane < HEAD_DIM).astype(f32).astype(bf16)
    high_lane = (lane >= HEAD_DIM).astype(f32).astype(bf16)

    def project(lhs, weight, gain, mask, store):
        for j in range(width // 256):
            u = jnp.dot(lhs, weight[:, j * 256 : (j + 1) * 256], preferred_element_type=f32)
            for t in range(2):
                tile = u[:, t * 128 : (t + 1) * 128]
                res = tile.astype(bf16) if gain is None else head_norm_tile(tile, gain)
                store(2 * j + t, res if mask is None else res * mask)

    def to_text(buf):
        def store(i, value):
            buf[i] = value

        return store

    def to_half(buf, half):
        def store(i, value):
            buf[i, half] = value

        return store

    text_lhs = text_norm[...].astype(bf16)
    loads[0].wait()
    project(text_lhs, wtext.at[0], gain_of(2), None, to_text(kt6))
    forward(3)
    forward(4)
    loads[1].wait()
    project(text_lhs, wtext.at[1], None, keep, to_text(vt6))
    for k in range(5, ring):
        forward(k)

    def norm_half(half):
        def block(i, carry):
            normed[half, i] = norm_rows(gathered[half, i].astype(f32), 0).astype(bf16)
            return carry

        lax.fori_loop(0, ring, block, 0, unroll=2)

    q_gain = gain_of(0) * (1.0 / math.sqrt(HEAD_DIM))
    k_gain = gain_of(1)

    def image_project(half):
        lhs = normed[half].reshape(own_rows, model)
        project(lhs, wqkv.at[1], k_gain, None, to_half(k6, half))
        project(lhs, wqkv.at[2], None, None, to_half(v6, half))
        project(lhs, wqkv.at[0], q_gain, None, to_half(q6, half))

    norm_half(m)
    for i in (2, 3, 4):
        loads[i].wait()
    image_project(m)
    for k in range(ring):
        src = lax.rem(s + ring - k, ring)
        pltpu.make_async_remote_copy(
            src_ref=gathered.at[other, src], dst_ref=gathered.at[other, src],
            send_sem=fwd_send.at[k], recv_sem=fwd_recv.at[k],
            device_id=partner, device_id_type=MESH).wait_recv()
    norm_half(other)
    image_project(other)

    def dot_t(a, b):
        return lax.dot_general(a, b, (((1,), (1,)), ((), ())), preferred_element_type=f32)

    def attend(half):
        for p in range(pairs):
            q, kt, vt = q6[p, half], kt6[p], vt6[p]
            k = k6[p].reshape(2 * own_rows, 128)
            v = v6[p].reshape(2 * own_rows, 128)
            outs = []
            for mine, rest in ((low_lane, high_lane), (high_lane, low_lane)):
                qh = q * mine
                w_img = jnp.exp(dot_t(qh, k)).astype(bf16)
                w_txt = jnp.exp(dot_t(qh, kt)).astype(bf16)
                outs.append(
                    jnp.dot(w_img, v * mine + rest, preferred_element_type=f32)
                    + jnp.dot(w_txt, vt * mine + keep * rest, preferred_element_type=f32))
            numer = jnp.where(lane < HEAD_DIM, outs[0], outs[1])
            denom = pltpu.roll(jnp.where(lane < HEAD_DIM, outs[1], outs[0]), HEAD_DIM, 1)
            attended[half, :, p * 128 : (p + 1) * 128] = (numer / denom).astype(bf16)

    def wide_dot(lhs, weight, out, half, first_at, count):
        for j in range(model // 512):
            cols = slice(j * 512, (j + 1) * 512)
            res = jnp.dot(lhs, weight[:, cols], preferred_element_type=f32).astype(bf16)
            out[half, first_at : first_at + count, :, cols] = res.reshape(count, rows, 512)

    batches = 2
    step = ring // batches

    def swap(src, dst, send, recv, h):
        at = pl.ds(h * step, step)
        cp = pltpu.make_async_remote_copy(
            src_ref=src.at[at], dst_ref=dst.at[at], send_sem=send.at[h], recv_sem=recv.at[h],
            device_id=partner, device_id_type=MESH)
        cp.start()
        sends.append(cp)
        return cp

    attend(other)
    loads[5].wait()
    wide_dot(attended[other], wout, part, other, 0, ring)
    rs = [swap(part.at[other], part_in, rs_send, rs_recv, h) for h in range(batches)]
    attend(m)
    wide_dot(attended[m], wout, part, m, 0, ring)

    def first_block(i, carry):
        total = part[m, i].astype(f32) + part_in[i].astype(f32)
        first = gathered[m, i].astype(f32) + mod_row(2) * total
        first_buf[i] = first
        mlp_in[m, i] = norm_rows(first, 3).astype(bf16)
        return carry

    ag = []
    for h in range(batches):
        rs[h].wait_recv()
        lax.fori_loop(h * step, (h + 1) * step, first_block, 0, unroll=2)
        ag.append(swap(mlp_in.at[m], mlp_in.at[m], ag_send, ag_recv, h))

    def up(half, first_at, count):
        lhs = mlp_in[half, first_at : first_at + count].reshape(count * rows, model)
        for j in range(units // 512):
            cols = slice(j * 512, (j + 1) * 512)
            r = jnp.dot(lhs, wup[:, cols], preferred_element_type=f32)
            inner = math.sqrt(2.0 / math.pi) * (r + 0.044715 * (r * r * r))
            value = (0.5 * r * (1.0 + jnp.tanh(inner))).astype(bf16)
            act[half, first_at : first_at + count, :, cols] = value.reshape(count, rows, 512)

    def down_rows(half, first_at, count):
        lhs = act[half, first_at : first_at + count].reshape(count * rows, units)
        wide_dot(lhs, wdown, down, half, first_at, count)

    loads[6].wait()
    loads[7].wait()
    up(m, 0, ring)
    loads[8].wait()
    loads[9].wait()
    dn = []
    for h in range(batches):
        ag[h].wait_recv()
        up(other, h * step, step)
        down_rows(other, h * step, step)
        dn.append(swap(down.at[other], down_in, dn_send, dn_recv, h))
    down_rows(m, 0, ring)

    def final_block(i, carry):
        total = down[m, i].astype(f32) + down_in[i].astype(f32)
        second = first_buf[i] + mod_row(5) * total
        final[i] = norm_rows(second, 8).astype(bf16)
        return carry

    head = whead_ref[...]
    heads2 = jnp.concatenate([head, head], axis=0)
    home = s // (ring // 2)
    slot = c * (ring // 2) + lax.rem(s, ring // 2)
    at_home = c == home
    outs = []
    for h in range(batches):
        dn[h].wait_recv()
        lax.fori_loop(h * step, (h + 1) * step, final_block, 0, unroll=2)
        hv = dot_t(final[h * step : (h + 1) * step].reshape(step * rows, model), heads2)
        half_out[h * step : (h + 1) * step] = hv.reshape(step, rows, 128)
        for dest in range(h * step, (h + 1) * step):
            outs.append(pltpu.make_async_remote_copy(
                src_ref=half_out.at[dest], dst_ref=half_in.at[slot],
                send_sem=out_send.at[dest], recv_sem=out_recv.at[slot],
                device_id=(home, dest, m), device_id_type=MESH))
            stays = jnp.logical_and(at_home, s == dest)

            @pl.when(jnp.logical_not(stays))
            def _(cp=outs[-1]):
                cp.start()

            @pl.when(stays)
            def _(dest=dest):
                half_in[slot] = half_out[dest]

    for q in range(ring):
        branch, local = q // (ring // 2), q % (ring // 2)
        prompt = c * (ring // 2) + local
        is_self = jnp.logical_and(c == branch, s == prompt)

        @pl.when(jnp.logical_not(is_self))
        def _():
            pltpu.make_async_remote_copy(
                src_ref=half_out.at[0], dst_ref=half_in.at[q],
                send_sem=out_send.at[0], recv_sem=out_recv.at[q],
                device_id=(branch, prompt, m), device_id_type=MESH).wait_recv()

    t = step_ref[...]

    def sigma(index):
        level = 1.0 - jnp.broadcast_to(index.astype(f32), (1, PATCH)) / STEPS
        return SHIFT * level / (1.0 + (SHIFT - 1.0) * level)

    now, after = sigma(t), sigma(t + 1)
    for p in range(ring // 2):
        cond = half_in[p][:, :PATCH]
        uncond = half_in[ring // 2 + p][:, :PATCH]
        velocity = uncond + GUIDE * (cond - uncond)
        base = latent_ref[:, p, :]
        out_ref[0, :, p, :] = velocity
        out_ref[1, :, p, :] = base + (after - now) * velocity
        out_ref[2, :, p, :] = base - now * velocity

    for cp in sends:
        cp.wait_send()

    for dest in range(ring):
        @pl.when(jnp.logical_not(jnp.logical_and(at_home, s == dest)))
        def _(cp=outs[dest]):
            cp.wait_send()


def fused_shards(
    image_hidden, text_hidden, modulation, text_lengths, timestep, latent,
    w_qkv, w_out, w_text_kv, norm_gain, w_up, w_down, w_head,
):
    f32, bf16 = jnp.float32, jnp.bfloat16
    rows, prompts, model = image_hidden.shape[1:]
    txt = text_hidden.shape[1]
    txt_pad = -(-txt // 16) * 16
    width = w_out.shape[0]
    units = w_up.shape[1]
    own_rows = rows * prompts
    pairs = width // 128
    chunks = 2
    vmem = pl.BlockSpec(memory_space=pltpu.VMEM)
    smem = pl.BlockSpec(memory_space=pltpu.SMEM)
    anym = pl.BlockSpec(memory_space=pl.ANY)
    dma = pltpu.SemaphoreType.DMA
    out = jax.ShapeDtypeStruct((3,) + latent.shape, f32)
    scratch = [
        pltpu.VMEM(w_qkv.shape, bf16), pltpu.VMEM(w_out.shape, bf16), pltpu.VMEM(w_text_kv.shape, bf16),
        pltpu.VMEM(w_up.shape, bf16), pltpu.VMEM(w_down.shape, bf16),
        pltpu.VMEM((model // 128, own_rows, 128), f32),
        pltpu.VMEM((prompts, rows, model), bf16),
        pltpu.VMEM((2, prompts, rows, model), bf16),
        pltpu.VMEM((2, prompts, rows, model), bf16),
        pltpu.VMEM((txt_pad, model), f32),
        pltpu.VMEM((pairs, 2, own_rows, 128), bf16),
        pltpu.VMEM((pairs, 2, own_rows, 128), bf16),
        pltpu.VMEM((pairs, 2, own_rows, 128), bf16),
        pltpu.VMEM((pairs, txt_pad, 128), bf16),
        pltpu.VMEM((pairs, txt_pad, 128), bf16),
        pltpu.VMEM((2, own_rows, width), bf16),
        pltpu.VMEM((2, prompts, rows, model), bf16),
        pltpu.VMEM((prompts, rows, model), bf16),
        pltpu.VMEM((prompts, rows, model), f32),
        pltpu.VMEM((2, prompts, rows, model), bf16),
        pltpu.VMEM((2, prompts, rows, units), bf16),
        pltpu.VMEM((2, prompts, rows, model), bf16),
        pltpu.VMEM((prompts, rows, model), bf16),
        pltpu.VMEM((prompts, rows, model), bf16),
        pltpu.VMEM((prompts, rows, 128), f32),
        pltpu.VMEM((prompts, rows, 128), f32),
        dma((10,)), dma((prompts,)), dma((prompts,)), dma((prompts,)), dma((prompts,)),
        dma((chunks,)), dma((chunks,)), dma((2,)), dma((2,)), dma((chunks,)), dma((chunks,)),
        dma((prompts,)), dma((prompts,)),
    ]
    stacked = pl.pallas_call(
        fused_kernel,
        out_shape=out,
        in_specs=[vmem, vmem, vmem, smem, vmem, vmem, anym, anym, anym, vmem, anym, anym, vmem],
        out_specs=vmem,
        scratch_shapes=scratch,
        compiler_params=pltpu.CompilerParams(
            collective_id=0, has_side_effects=True, vmem_limit_bytes=60 << 20),
        name="fused_block",
    )(
        image_hidden[0], text_hidden[0], jnp.transpose(modulation[0], (1, 0, 2)), text_lengths,
        timestep.reshape(1, 1), latent, w_qkv, w_out, w_text_kv, norm_gain, w_up, w_down, jnp.transpose(w_head),
    )
    return stacked[0], stacked[1], stacked[2]


def solution(mesh):
    placed = (
        P("cfg", ("seq", "mlp"), None, None),
        P("cfg", "seq", None),
        P("cfg", None, None, None),
        P("cfg", None),
        P(),
        P(("seq", "mlp"), "cfg", None),
        P(None, None, "mlp"),
        P("mlp", None),
        P(None, None, "mlp"),
        P(),
        P(None, "mlp"),
        P("mlp", None),
        P(),
    )
    fits = mesh.shape["cfg"] == 2 and mesh.shape["seq"] == PROMPTS and mesh.shape["mlp"] == 2
    return jax.shard_map(
        fused_shards if fits else shards,
        mesh=mesh,
        in_specs=placed,
        out_specs=(
            P(("seq", "mlp"), "cfg", None),
            P(("seq", "mlp"), "cfg", None),
            P(("seq", "mlp"), "cfg", None),
        ),
        check_vma=False,
    )
```
